256 devices in a mesh: tm: 64 (over y, x, z_lo), agent: 4 (over z_hi, core).
Axes of the slice: x: 4, y: 4, z: 8 (z_hi: 2, z_lo: 4; z = z_hi * 4 + z_lo), core: 2. Of those that a mesh axis runs over, the one named last changes fastest.
Arguments:
- panel: bfloat16 [16384, 64, 128], P('tm', 'agent'), may hold values from -6 to 6
- w_tqkv: bfloat16 [128, 384], replicated, as said below
- w_tout: bfloat16 [128, 128], replicated, may hold values from -0.5 to 0.5
- w_cqkv: bfloat16 [128, 384], replicated, as said below
- w_cout: bfloat16 [128, 128], replicated, may hold values from -0.5 to 0.5
Outputs:
- block_out: bfloat16 [16384, 64, 128], P('tm', 'agent')
The draws below stay inside these ranges and needn't reach their ends.
Inputs may be any that keep to these rules, and one draw needn't show every extreme that they name: `w_tqkv`: query, key and value weights with entries of order 128 ** -0.5, up to some tens of times that in query columns. `w_cqkv`: query, key and value weights with entries of order 128 ** -0.5, up to some tens of times that in query columns.
All inputs are finite; a program needn't handle non-finite values.
Results may differ from the reference program's by a relative error of at most 0.0045.
The reference program's roundings to bfloat16 on the way count: a program that leaves them out, or rounds other values in their place, can miss the bound.
Values may be sent and summed in bfloat16 or wider, within the bound.
A program may use at most 64 MiB of HBM per device.

```python
import jax
import jax.numpy as jnp
from jax import lax

D = 128
HEADS = 4
WINDOW = 256
TM_DEV = 256
TIME = 16384
AGENTS = 64


def qkv_weights(key):
    first, second, third = jax.random.split(key, 3)
    spread = D ** (-0.5)
    w_query = jnp.clip(jax.random.normal(first, (D, D), jnp.float32), -5.0, 5.0) * spread
    w_value = jnp.clip(jax.random.normal(third, (D, D), jnp.float32), -5.0, 5.0) * spread
    noise = jnp.clip(jax.random.normal(second, (D, D), jnp.float32), -5.0, 5.0) * spread
    w_key = noise
    return jnp.concatenate([w_query, w_key, w_value], 1)


def draw_w_tqkv(key, part):
    return qkv_weights(jax.random.fold_in(key, 11)).astype(jnp.bfloat16)


def draw_w_cqkv(key, part):
    return qkv_weights(jax.random.fold_in(key, 23)).astype(jnp.bfloat16)


def levels(key, shape, cuts, smallest, top_value):
    level = 1.0
    for axis_at, parts in cuts:
        heights = jax.random.uniform(jax.random.fold_in(jax.random.fold_in(key, 6), axis_at), (parts,), jnp.float32, smallest / len(cuts), top_value / len(cuts))
        level = level * jnp.repeat(jnp.exp(heights), shape[axis_at] // parts).reshape((-1,) + (1,) * (len(shape) - 1 - axis_at))
    return level


def normal_values(stream_key, shape, deviation, limit, pieces=(), held_as=jnp.bfloat16):
    values = deviation * jax.random.normal(stream_key, shape, jnp.float32)
    if pieces:
        values = values * levels(stream_key, shape, pieces, -0.22, 0.18)
    return jnp.clip(values, -limit, limit).astype(held_as)


def setup_inputs(seed: int = 0) -> dict:
    seeds = jax.random.split(jax.random.key(seed), 6)
    panel = normal_values(seeds[0], (TIME, AGENTS, D), 1.0, 6.0, ((0, 64), (1, 4)))
    w_tqkv = draw_w_tqkv(jax.random.fold_in(seeds[5], 71), 0)
    w_tout = normal_values(seeds[2], (D, D), D ** -0.5, 0.5)
    w_cqkv = draw_w_cqkv(jax.random.fold_in(seeds[5], 71), 0)
    w_cout = normal_values(seeds[4], (D, D), D ** -0.5, 0.5)
    return dict(panel=panel, w_tqkv=w_tqkv, w_tout=w_tout, w_cqkv=w_cqkv, w_cout=w_cout)


epsilon = 1e-06

def normalize(values):
    widened = values.astype(jnp.float32)
    scale = lax.rsqrt(lax.optimization_barrier(jnp.mean(widened * widened, axis=-1, keepdims=True)) + epsilon)
    return (widened * scale).astype(jnp.bfloat16)

def project(normed, weight):
    shape = normed.shape
    result = jnp.dot(normed.reshape(-1, shape[-1]), weight, preferred_element_type=jnp.float32)
    return result.astype(jnp.bfloat16).reshape(shape[:-1] + (weight.shape[1],))

def softmax_rows(scores):
    top = lax.optimization_barrier(jnp.max(scores, axis=-1, keepdims=True))
    expo = jnp.exp(scores - top)
    return (expo / lax.optimization_barrier(jnp.sum(expo, axis=-1, keepdims=True))).astype(jnp.bfloat16)

def temporal_agent(qkv_rows):
    width = qkv_rows.shape[1] // 3
    head_size = width // HEADS
    prior_count = WINDOW // TM_DEV
    nblocks = TIME // TM_DEV
    queries = qkv_rows[:, :width].reshape(nblocks, TM_DEV, HEADS, head_size)
    padded = jnp.concatenate([jnp.zeros((WINDOW, 2 * width), jnp.bfloat16), qkv_rows[:, width:]], 0)
    padded = padded.reshape(nblocks + prior_count, TM_DEV, 2 * width)
    key_rows = jnp.concatenate([padded[idx:idx + nblocks] for idx in range(prior_count + 1)], 1)
    span = key_rows.shape[1]
    keyset = key_rows[..., :width].reshape(nblocks, span, HEADS, head_size)
    valset = key_rows[..., width:].reshape(nblocks, span, HEADS, head_size)
    scores = jnp.einsum('bqhe,bkhe->bhqk', queries.astype(jnp.float32), keyset.astype(jnp.float32)) * head_size ** (-0.5)
    rows_at = jnp.arange(TM_DEV)[None, :, None]
    cols_at = jnp.arange(span)[None, None, :]
    block_at = jnp.arange(nblocks)[:, None, None]
    allowed = (cols_at - WINDOW <= rows_at) & (cols_at > rows_at) & (block_at * TM_DEV + cols_at - WINDOW >= 0)
    scores = jnp.where(allowed[:, None], scores, -jnp.inf)
    weights = softmax_rows(scores)
    attended = jnp.einsum('bhqk,bkhe->bqhe', weights.astype(jnp.float32), valset.astype(jnp.float32))
    return attended.astype(jnp.bfloat16).reshape(TIME, width)

def cross_step(qkv_rows):
    width = qkv_rows.shape[1] // 3
    head_size = width // HEADS
    count = qkv_rows.shape[0]
    queries = qkv_rows[:, :width].reshape(count, HEADS, head_size).astype(jnp.float32)
    keyset = qkv_rows[:, width:2 * width].reshape(count, HEADS, head_size).astype(jnp.float32)
    valset = qkv_rows[:, 2 * width:].reshape(count, HEADS, head_size).astype(jnp.float32)
    scores = jnp.einsum('qhe,khe->hqk', queries, keyset) * head_size ** (-0.5)
    weights = softmax_rows(scores)
    attended = jnp.einsum('hqk,khe->qhe', weights.astype(jnp.float32), valset)
    return attended.astype(jnp.bfloat16).reshape(count, width)

def residual_add(base, attended, weight):
    update = jnp.dot(attended.reshape(-1, attended.shape[-1]), weight, preferred_element_type=jnp.float32)
    return (base.astype(jnp.float32) + update.reshape(base.shape)).astype(jnp.bfloat16)

def reference(panel, w_tqkv, w_tout, w_cqkv, w_cout):
    qkv_first = project(normalize(panel), w_tqkv)
    temporal = lax.map(temporal_agent, jnp.swapaxes(qkv_first, 0, 1))
    temporal = jnp.swapaxes(temporal, 0, 1)
    mixed = residual_add(panel, temporal, w_tout)
    qkv_second = project(normalize(mixed), w_cqkv)
    across = lax.map(cross_step, qkv_second)
    return residual_add(mixed, across, w_cout)
```

```python
import functools
import math

import jax
import jax.numpy as jnp
from jax import lax
from jax.experimental import pallas as pl
from jax.experimental.pallas import tpu as pltpu
from jax.sharding import PartitionSpec as P

HEADS = 4
WINDOW = 256
EPSILON = 1e-06
UNROLL = 4
PARTS = 2
BLOCK = 4
BLOCKS = 2
MESH = pl.DeviceIdType.MESH
NT = (((1,), (1,)), ((), ()))
NN = (((1,), (0,)), ((), ()))


def matmul(left, right, dims=NN):
    return lax.dot_general(left, right, dims, preferred_element_type=jnp.float32)


def normalized(values):
    widened = values.astype(jnp.float32)
    scale = lax.rsqrt(jnp.mean(widened * widened, axis=-1, keepdims=True) + EPSILON)
    return (widened * scale).astype(jnp.bfloat16)


def by_head(values, masks):
    return jnp.concatenate([values * mask for mask in masks], axis=0)


def pick_heads(stacked, rows, picks):
    blocks = [stacked[h * rows : (h + 1) * rows] for h in range(HEADS)]
    result = blocks[-1]
    for pick, block in zip(picks, blocks):
        result = jnp.where(pick, block, result)
    return result


def kernel(
    x_hbm, wt_hbm, wto_hbm, wc_hbm, wco_hbm, out_hbm,
    xv, halo, wt, wto, wc, wco, wide, q1, k1, v1, upd, mixed, slab, wvt, own_out, sib_out,
    load_sem, halo_send, halo_recv, mix_send, mix_recv, res_send, res_recv, store_sem,
    *, tm_axis, agent_axis, chunk,
):
    tm_dev, ag_dev, width = xv.shape
    chunks = tm_dev // chunk
    half = chunk // 2
    part = half // PARTS
    pieces = chunks * PARTS
    agents = slab.shape[1]
    pair = 2 * ag_dev
    head_size = width // HEADS
    factor = math.log2(math.e) * head_size ** (-0.5)
    tm = lax.axis_index(tm_axis)
    ag = lax.axis_index(agent_axis)
    tm_count = lax.axis_size(tm_axis)
    side = ag // 2
    core = ag % 2
    ahead = (lax.rem(tm + 1, tm_count), ag)
    behind = (lax.rem(tm + tm_count - 1, tm_count), ag)
    sibling = (tm, side * 2 + 1 - core)
    far = [(tm, (1 - side) * 2 + j) for j in range(2)]

    loads = [
        pltpu.make_async_copy(src, dst, load_sem.at[i])
        for i, (src, dst) in enumerate(
            [(x_hbm, xv), (wt_hbm, wt), (wto_hbm, wto), (wc_hbm, wc), (wco_hbm, wco)]
        )
    ]
    for load in loads:
        load.start()

    barrier = pltpu.get_barrier_semaphore()
    for peer in (ahead, behind, sibling, far[0], far[1]):
        pl.semaphore_signal(barrier, inc=1, device_id=peer, device_id_type=MESH)
    pl.semaphore_wait(barrier, 5)

    def halo_copy(c):
        rows = pl.ds(c * chunk, chunk)
        return pltpu.make_async_remote_copy(
            src_ref=x_hbm.at[rows], dst_ref=halo.at[rows],
            send_sem=halo_send.at[c], recv_sem=halo_recv.at[c],
            device_id=ahead, device_id_type=MESH,
        )

    for c in reversed(range(chunks)):
        halo_copy(c).start()

    lanes = lax.broadcasted_iota(jnp.int32, (1, width), 1) // head_size
    masks = [(lanes == h).astype(jnp.bfloat16) for h in range(HEADS)]
    picks = [lanes == h for h in range(HEADS - 1)]
    later = (
        lax.broadcasted_iota(jnp.int32, (HEADS * chunk, 128), 1)
        <= lax.broadcasted_iota(jnp.int32, (HEADS * chunk, 128), 0) % chunk
    )

    for load in loads[:2]:
        load.wait()

    group = 4

    def spread(src, start):
        def piece(i, carry):
            rows = normalized(src[pl.ds(start + i * 8, 8)].reshape(8 * ag_dev, width))
            wide[pl.ds(pl.multiple_of(i * 8 * ag_dev, 8 * ag_dev), 8 * ag_dev), :] = rows.astype(jnp.float32)
            return carry

        lax.fori_loop(0, chunk // 8, piece, 0)

    def project(row0, is_halo, start):
        def agents4(g, carry):
            parts = []
            for i in range(group):
                rows = wide[pl.ds(g * group + i, chunk, stride=ag_dev), :]
                parts.append(rows.astype(jnp.bfloat16))
            result = matmul(jnp.concatenate(parts, 0), wt[...])
            keys = result[:, width : 2 * width].astype(jnp.bfloat16)
            vals = result[:, 2 * width :].astype(jnp.bfloat16)
            at = pl.ds(g * group, group)
            k1[at, pl.ds(row0, chunk), :] = keys.reshape(group, chunk, width)
            v1[at, pl.ds(row0, chunk), :] = vals.reshape(group, chunk, width)
            if not is_halo:
                q1[at, pl.ds(start, chunk), :] = result[:, :width].astype(jnp.bfloat16).reshape(group, chunk, width)
            return carry

        lax.fori_loop(0, ag_dev // group, agents4, 0)

    extra = k1.shape[1] - 2 * tm_dev
    if extra:
        k1[:, pl.ds(2 * tm_dev, extra), :] = jnp.zeros((ag_dev, extra, width), jnp.bfloat16)
        v1[:, pl.ds(2 * tm_dev, extra), :] = jnp.zeros((ag_dev, extra, width), jnp.bfloat16)

    def own_chunk(c, carry):
        start = pl.multiple_of(c * chunk, chunk)
        spread(xv, start)
        project(pl.multiple_of(tm_dev + start, chunk), False, start)
        return carry

    lax.fori_loop(0, chunks, own_chunk, 0)
    for load in loads[2:]:
        load.wait()

    def mix_copies(k, p):
        start = (chunks - 1 - k) * chunk + p * part
        piece = k * PARTS + p
        away = pl.multiple_of(pair + core * ag_dev, ag_dev)
        result = []
        for i, (peer, target, slot) in enumerate(
            [(sibling, 1 - core, ag_dev), (far[0], 0, away), (far[1], 1, away)]
        ):
            result.append(
                pltpu.make_async_remote_copy(
                    src_ref=mixed.at[pl.ds(start + target * half, part)],
                    dst_ref=slab.at[pl.ds(piece * part, part), pl.ds(slot, ag_dev)],
                    send_sem=mix_send.at[piece, i],
                    recv_sem=mix_recv.at[piece, 0 if i == 0 else 1 + core],
                    device_id=peer, device_id_type=MESH,
                )
            )
        return result

    def mix_arrivals(piece):
        return [
            pltpu.make_async_remote_copy(
                src_ref=mixed.at[pl.ds(0, part)],
                dst_ref=slab.at[pl.ds(piece * part, part), pl.ds((i + 1) * ag_dev, ag_dev)],
                send_sem=mix_send.at[piece, i], recv_sem=mix_recv.at[piece, i],
                device_id=peer, device_id_type=MESH,
            )
            for i, peer in enumerate([sibling, far[0], far[1]])
        ]

    def temporal_chunk(k, carry):
        c = chunks - 1 - k
        start = pl.multiple_of(c * chunk, chunk)
        halo_copy(c).wait_recv()
        spread(halo, start)
        project(start, True, start)

        columns = lax.broadcasted_iota(jnp.int32, (1, WINDOW), 1) + start
        absent = jnp.where((tm == 0) & (columns < WINDOW), -1e30, 0.0)

        def temporal_agents(i, inner):
            ids = [i * UNROLL + j for j in range(UNROLL)]
            scores = [
                matmul(by_head(q1[a, pl.ds(start, chunk), :], masks), k1[a, pl.ds(start, WINDOW + 128), :], NT)
                for a in ids
            ]
            weights = []
            for score in scores:
                edge = jnp.where(later, score[:, WINDOW:], score[:, :128] + absent[:, :128])
                middle = score[:, 128:WINDOW] + absent[:, 128:]
                top = jnp.max(jnp.maximum(edge, middle), axis=1, keepdims=True)
                edge = jnp.exp2((edge - top) * factor)
                middle = jnp.exp2((middle - top) * factor)
                share = 1.0 / jnp.sum(edge + middle, axis=1, keepdims=True)
                edge = edge * share
                middle = middle * share
                weights.append(
                    jnp.concatenate(
                        [jnp.where(later, 0.0, edge), middle, jnp.where(later, edge, 0.0)], axis=1
                    ).astype(jnp.bfloat16)
                )
            sums = [matmul(weight, v1[a, pl.ds(start, WINDOW + 128), :]) for a, weight in zip(ids, weights)]
            attended = [pick_heads(value, chunk, picks).astype(jnp.bfloat16) for value in sums]
            update = matmul(jnp.concatenate(attended, 0), wto[...])
            for j, a in enumerate(ids):
                upd[pl.ds(a, chunk, stride=ag_dev), :] = update[j * chunk : (j + 1) * chunk]
            return inner

        lax.fori_loop(0, ag_dev // UNROLL, temporal_agents, 0)

        def add_piece(i, inner):
            rows = pl.ds(start + i * 8, 8)
            update = upd[pl.ds(pl.multiple_of(i * 8 * ag_dev, 8 * ag_dev), 8 * ag_dev), :]
            mixed[rows] = (xv[rows].astype(jnp.float32) + update.reshape(8, ag_dev, width)).astype(jnp.bfloat16)
            return inner

        lax.fori_loop(0, chunk // 8, add_piece, 0)
        slab[pl.ds(k * half, half), pl.ds(0, ag_dev), :] = mixed[pl.ds(start + core * half, half)]
        for p in range(PARTS):
            for copy in mix_copies(k, p):
                copy.start()
        return carry

    lax.fori_loop(0, chunks, temporal_chunk, 0)

    def result_copy(piece, owner):
        start = (chunks - 1 - piece // PARTS) * chunk + owner * half + piece % PARTS * part
        return pltpu.make_async_remote_copy(
            src_ref=sib_out.at[pl.ds(piece * part, part)], dst_ref=out_hbm.at[pl.ds(start, part)],
            send_sem=res_send.at[piece], recv_sem=res_recv.at[piece],
            device_id=sibling, device_id_type=MESH,
        )

    def store_copy(piece):
        start = (chunks - 1 - piece // PARTS) * chunk + core * half + piece % PARTS * part
        return pltpu.make_async_copy(
            own_out.at[pl.ds(piece * part, part)], out_hbm.at[pl.ds(start, part)], store_sem.at[piece]
        )

    blocks = lax.broadcasted_iota(jnp.int32, (1, width), 1) // pair
    none = jnp.zeros((agents, width), jnp.bfloat16)

    def cross_block(first):
        rows = slab[pl.ds(first, BLOCK)]
        normed = normalized(rows.reshape(BLOCK * agents, width))
        keys = matmul(normed, wc[:, width : 2 * width]).astype(jnp.bfloat16)
        values = matmul(wvt[...], normed, NT).astype(jnp.bfloat16)
        own = normed.reshape(BLOCK, agents, width)[:, :pair].reshape(BLOCK * pair, width)
        queries = matmul(own, wc[:, :width]).astype(jnp.bfloat16)
        weights = []
        for t in range(BLOCK):
            query = queries[t * pair : (t + 1) * pair]
            stacked = jnp.concatenate([query * masks[(place - t) % HEADS] for place in range(HEADS)], axis=0)
            scores = matmul(keys[t * agents : (t + 1) * agents], stacked, NT)
            powers = jnp.exp2((scores - jnp.max(scores, axis=0, keepdims=True)) * factor)
            share = 1.0 / jnp.sum(powers, axis=0, keepdims=True)
            weights.append((powers * share).astype(jnp.bfloat16))
        sums = []
        for t in range(0, BLOCK, 2):
            both = jnp.concatenate(
                [
                    jnp.concatenate([weights[t], none], axis=1),
                    jnp.concatenate([none, weights[t + 1]], axis=1),
                ],
                axis=0,
            )
            result = matmul(values[:, t * agents : (t + 2) * agents], both)
            sums += [result[:, :width], result[:, width:]]
        heads = []
        for h in range(HEADS):
            band = [value[h * head_size : (h + 1) * head_size] for value in sums]
            result = band[(HEADS - 1 - h) % HEADS]
            for place in range(HEADS - 1):
                result = jnp.where(blocks == place, band[(place - h) % HEADS], result)
            heads.append(pltpu.roll(result, width - h * pair, 1) if h else result)
        attended = jnp.concatenate(heads, axis=0).T.astype(jnp.bfloat16)
        update = matmul(attended, wco[...]).reshape(BLOCK, pair, width)
        final = (rows[:, :pair].astype(jnp.float32) + update).astype(jnp.bfloat16)
        own_out[pl.ds(first, BLOCK)] = final[:, :ag_dev]
        sib_out[pl.ds(first, BLOCK)] = final[:, ag_dev:]

    def cross_piece(piece, carry):
        for copy in mix_arrivals(piece):
            copy.wait_recv()

        def cross_blocks(i, inner):
            for j in range(BLOCKS):
                cross_block(piece * part + (i * BLOCKS + j) * BLOCK)
            return inner

        lax.fori_loop(0, part // (BLOCK * BLOCKS), cross_blocks, 0)
        result_copy(piece, core).start()
        store_copy(piece).start()
        return carry

    wvt[...] = wc[:, 2 * width :].astype(jnp.float32).T.astype(jnp.bfloat16)
    lax.fori_loop(0, pieces, cross_piece, 0)

    def drain(k, carry):
        halo_copy(k).wait_send()
        for p in range(PARTS):
            for copy in mix_copies(k, p):
                copy.wait_send()
            piece = k * PARTS + p
            result_copy(piece, core).wait_send()
            result_copy(piece, 1 - core).wait_recv()
            store_copy(piece).wait()
        return carry

    lax.fori_loop(0, chunks, drain, 0)


def local(panel, w_tqkv, w_tout, w_cqkv, w_cout):
    tm_dev, ag_dev, width = panel.shape
    chunk = 64
    chunks = tm_dev // chunk
    half = chunk // 2
    pieces = chunks * PARTS
    agents = ag_dev * lax.axis_size("agent")
    rows = WINDOW + tm_dev + (128 - chunk)
    bf16, f32 = jnp.bfloat16, jnp.float32
    any_spec = pl.BlockSpec(memory_space=pl.ANY)
    return pl.pallas_call(
        functools.partial(kernel, tm_axis="tm", agent_axis="agent", chunk=chunk),
        out_shape=jax.ShapeDtypeStruct(panel.shape, bf16),
        in_specs=[any_spec] * 5,
        out_specs=any_spec,
        scratch_shapes=[
            pltpu.VMEM(panel.shape, bf16),
            pltpu.VMEM(panel.shape, bf16),
            pltpu.VMEM(w_tqkv.shape, bf16),
            pltpu.VMEM(w_tout.shape, bf16),
            pltpu.VMEM(w_cqkv.shape, bf16),
            pltpu.VMEM(w_cout.shape, bf16),
            pltpu.VMEM((chunk * ag_dev, width), f32),
            pltpu.VMEM((ag_dev, tm_dev, width), bf16),
            pltpu.VMEM((ag_dev, rows, width), bf16),
            pltpu.VMEM((ag_dev, rows, width), bf16),
            pltpu.VMEM((chunk * ag_dev, width), f32),
            pltpu.VMEM(panel.shape, bf16),
            pltpu.VMEM((chunks * half, agents, width), bf16),
            pltpu.VMEM((width, width), bf16),
            pltpu.VMEM((chunks * half, ag_dev, width), bf16),
            pltpu.VMEM((chunks * half, ag_dev, width), bf16),
            pltpu.SemaphoreType.DMA((5,)),
            pltpu.SemaphoreType.DMA((chunks,)),
            pltpu.SemaphoreType.DMA((chunks,)),
            pltpu.SemaphoreType.DMA((pieces, 3)),
            pltpu.SemaphoreType.DMA((pieces, 3)),
            pltpu.SemaphoreType.DMA((pieces,)),
            pltpu.SemaphoreType.DMA((pieces,)),
            pltpu.SemaphoreType.DMA((pieces,)),
        ],
        compiler_params=pltpu.CompilerParams(
            collective_id=0, has_side_effects=True, vmem_limit_bytes=56 * 2**20
        ),
        name="axial_block",
    )(panel, w_tqkv, w_tout, w_cqkv, w_cout)


def solution(mesh):
    in_specs = (P("tm", "agent", None), P(), P(), P(), P())
    out_specs = P("tm", "agent", None)
    return jax.shard_map(local, mesh=mesh, in_specs=in_specs, out_specs=out_specs, check_vma=False)
```

```python
import functools
import math

import jax
import jax.numpy as jnp
from jax import lax
from jax.experimental import pallas as pl
from jax.experimental.pallas import tpu as pltpu
from jax.sharding import PartitionSpec as P

HEADS = 4
WINDOW = 256
EPSILON = 1e-06
UNROLL = 4
PARTS = 2
BLOCK = 4
BLOCKS = 4
MESH = pl.DeviceIdType.MESH
NT = (((1,), (1,)), ((), ()))
NN = (((1,), (0,)), ((), ()))


def matmul(left, right, dims=NN):
    return lax.dot_general(left, right, dims, preferred_element_type=jnp.float32)


def normalized(values):
    widened = values.astype(jnp.float32)
    scale = lax.rsqrt(jnp.mean(widened * widened, axis=-1, keepdims=True) + EPSILON)
    return (widened * scale).astype(jnp.bfloat16)


def by_head(values, masks):
    return jnp.concatenate([values * mask for mask in masks], axis=0)


def pick_heads(stacked, rows, picks):
    blocks = [stacked[h * rows : (h + 1) * rows] for h in range(HEADS)]
    result = blocks[-1]
    for pick, block in zip(picks, blocks):
        result = jnp.where(pick, block, result)
    return result


def kernel(
    x_hbm, wt_hbm, wto_hbm, wc_hbm, wco_hbm, out,
    xv, halo, wt, wto, wc, wco, wide, q1, k1, v1, upd, mixed, slab, wvt, sib_out,
    load_sem, halo_send, halo_recv, mix_send, mix_recv, res_send, res_recv,
    *, tm_axis, agent_axis, chunk,
):
    tm_dev, ag_dev, width = xv.shape
    chunks = tm_dev // chunk
    half = chunk // 2
    part = half // PARTS
    pieces = chunks * PARTS
    agents = slab.shape[1]
    pair = 2 * ag_dev
    head_size = width // HEADS
    factor = math.log2(math.e) * head_size ** (-0.5)
    tm = lax.axis_index(tm_axis)
    ag = lax.axis_index(agent_axis)
    tm_count = lax.axis_size(tm_axis)
    side = ag // 2
    core = ag % 2
    ahead = (lax.rem(tm + 1, tm_count), ag)
    behind = (lax.rem(tm + tm_count - 1, tm_count), ag)
    sibling = (tm, side * 2 + 1 - core)
    far = [(tm, (1 - side) * 2 + j) for j in range(2)]

    loads = [
        pltpu.make_async_copy(src, dst, load_sem.at[i])
        for i, (src, dst) in enumerate(
            [(x_hbm, xv), (wt_hbm, wt), (wto_hbm, wto), (wc_hbm, wc), (wco_hbm, wco)]
        )
    ]
    for load in loads:
        load.start()

    barrier = pltpu.get_barrier_semaphore()
    for peer in (ahead, behind, sibling, far[0], far[1]):
        pl.semaphore_signal(barrier, inc=1, device_id=peer, device_id_type=MESH)
    pl.semaphore_wait(barrier, 5)

    def halo_copy(c):
        rows = pl.ds(c * chunk, chunk)
        return pltpu.make_async_remote_copy(
            src_ref=x_hbm.at[rows], dst_ref=halo.at[rows],
            send_sem=halo_send.at[c], recv_sem=halo_recv.at[c],
            device_id=ahead, device_id_type=MESH,
        )

    for c in reversed(range(chunks)):
        halo_copy(c).start()

    lanes = lax.broadcasted_iota(jnp.int32, (1, width), 1) // head_size
    masks = [(lanes == h).astype(jnp.bfloat16) for h in range(HEADS)]
    picks = [lanes == h for h in range(HEADS - 1)]
    later = (
        lax.broadcasted_iota(jnp.int32, (HEADS * chunk, 128), 1)
        <= lax.broadcasted_iota(jnp.int32, (HEADS * chunk, 128), 0) % chunk
    )

    for load in loads[:2]:
        load.wait()

    group = 4

    def spread(src, start):
        def piece(i, carry):
            rows = normalized(src[pl.ds(start + i * 8, 8)].reshape(8 * ag_dev, width))
            wide[pl.ds(pl.multiple_of(i * 8 * ag_dev, 8 * ag_dev), 8 * ag_dev), :] = rows.astype(jnp.float32)
            return carry

        lax.fori_loop(0, chunk // 8, piece, 0)

    def project(row0, is_halo, start):
        def agents4(g, carry):
            parts = []
            for i in range(group):
                rows = wide[pl.ds(g * group + i, chunk, stride=ag_dev), :]
                parts.append(rows.astype(jnp.bfloat16))
            result = matmul(jnp.concatenate(parts, 0), wt[...])
            keys = result[:, width : 2 * width].astype(jnp.bfloat16)
            vals = result[:, 2 * width :].astype(jnp.bfloat16)
            at = pl.ds(g * group, group)
            k1[at, pl.ds(row0, chunk), :] = keys.reshape(group, chunk, width)
            v1[at, pl.ds(row0, chunk), :] = vals.reshape(group, chunk, width)
            if not is_halo:
                q1[at, pl.ds(start, chunk), :] = result[:, :width].astype(jnp.bfloat16).reshape(group, chunk, width)
            return carry

        lax.fori_loop(0, ag_dev // group, agents4, 0)

    extra = k1.shape[1] - 2 * tm_dev
    if extra:
        k1[:, pl.ds(2 * tm_dev, extra), :] = jnp.zeros((ag_dev, extra, width), jnp.bfloat16)
        v1[:, pl.ds(2 * tm_dev, extra), :] = jnp.zeros((ag_dev, extra, width), jnp.bfloat16)

    def own_chunk(c, carry):
        start = pl.multiple_of(c * chunk, chunk)
        spread(xv, start)
        project(pl.multiple_of(tm_dev + start, chunk), False, start)
        return carry

    lax.fori_loop(0, chunks, own_chunk, 0)
    for load in loads[2:]:
        load.wait()

    def mix_copies(k, p):
        start = (chunks - 1 - k) * chunk + p * part
        piece = k * PARTS + p
        away = pl.multiple_of(pair + core * ag_dev, ag_dev)
        result = []
        for i, (peer, target, slot) in enumerate(
            [(sibling, 1 - core, ag_dev), (far[0], 0, away), (far[1], 1, away)]
        ):
            result.append(
                pltpu.make_async_remote_copy(
                    src_ref=mixed.at[pl.ds(start + target * half, part)],
                    dst_ref=slab.at[pl.ds(piece * part, part), pl.ds(slot, ag_dev)],
                    send_sem=mix_send.at[piece, i],
                    recv_sem=mix_recv.at[piece, 0 if i == 0 else 1 + core],
                    device_id=peer, device_id_type=MESH,
                )
            )
        return result

    def mix_arrivals(piece):
        return [
            pltpu.make_async_remote_copy(
                src_ref=mixed.at[pl.ds(0, part)],
                dst_ref=slab.at[pl.ds(piece * part, part), pl.ds((i + 1) * ag_dev, ag_dev)],
                send_sem=mix_send.at[piece, i], recv_sem=mix_recv.at[piece, i],
                device_id=peer, device_id_type=MESH,
            )
            for i, peer in enumerate([sibling, far[0], far[1]])
        ]

    def temporal_chunk(k, carry):
        c = chunks - 1 - k
        start = pl.multiple_of(c * chunk, chunk)
        halo_copy(c).wait_recv()
        spread(halo, start)
        project(start, True, start)

        columns = lax.broadcasted_iota(jnp.int32, (1, WINDOW), 1) + start
        absent = jnp.where((tm == 0) & (columns < WINDOW), -1e30, 0.0)

        def temporal_agents(i, inner):
            ids = [i * UNROLL + j for j in range(UNROLL)]
            scores = [
                matmul(by_head(q1[a, pl.ds(start, chunk), :], masks), k1[a, pl.ds(start, WINDOW + 128), :], NT)
                for a in ids
            ]
            weights = []
            for score in scores:
                edge = jnp.where(later, score[:, WINDOW:], score[:, :128] + absent[:, :128])
                middle = score[:, 128:WINDOW] + absent[:, 128:]
                top = jnp.max(jnp.maximum(edge, middle), axis=1, keepdims=True)
                edge = jnp.exp2((edge - top) * factor)
                middle = jnp.exp2((middle - top) * factor)
                share = 1.0 / jnp.sum(edge + middle, axis=1, keepdims=True)
                edge = edge * share
                middle = middle * share
                weights.append(
                    jnp.concatenate(
                        [jnp.where(later, 0.0, edge), middle, jnp.where(later, edge, 0.0)], axis=1
                    ).astype(jnp.bfloat16)
                )
            sums = [matmul(weight, v1[a, pl.ds(start, WINDOW + 128), :]) for a, weight in zip(ids, weights)]
            attended = [pick_heads(value, chunk, picks).astype(jnp.bfloat16) for value in sums]
            update = matmul(jnp.concatenate(attended, 0), wto[...])
            for j, a in enumerate(ids):
                upd[pl.ds(a, chunk, stride=ag_dev), :] = update[j * chunk : (j + 1) * chunk]
            return inner

        lax.fori_loop(0, ag_dev // UNROLL, temporal_agents, 0)

        def add_piece(i, inner):
            rows = pl.ds(start + i * 8, 8)
            update = upd[pl.ds(pl.multiple_of(i * 8 * ag_dev, 8 * ag_dev), 8 * ag_dev), :]
            mixed[rows] = (xv[rows].astype(jnp.float32) + update.reshape(8, ag_dev, width)).astype(jnp.bfloat16)
            return inner

        lax.fori_loop(0, chunk // 8, add_piece, 0)
        slab[pl.ds(k * half, half), pl.ds(0, ag_dev), :] = mixed[pl.ds(start + core * half, half)]
        for p in range(PARTS):
            for copy in mix_copies(k, p):
                copy.start()
        return carry

    lax.fori_loop(0, chunks, temporal_chunk, 0)

    def result_copy(piece, owner):
        start = (chunks - 1 - piece // PARTS) * chunk + owner * half + piece % PARTS * part
        return pltpu.make_async_remote_copy(
            src_ref=sib_out.at[pl.ds(piece * part, part)], dst_ref=out.at[pl.ds(start, part)],
            send_sem=res_send.at[piece], recv_sem=res_recv.at[piece],
            device_id=sibling, device_id_type=MESH,
        )

    blocks = lax.broadcasted_iota(jnp.int32, (1, width), 1) // pair
    none = jnp.zeros((agents, width), jnp.bfloat16)

    def softmax_columns(scores):
        powers = jnp.exp2((scores - jnp.max(scores, axis=0, keepdims=True)) * factor)
        share = 1.0 / jnp.sum(powers, axis=0, keepdims=True)
        return (powers * share).astype(jnp.bfloat16)

    def pair_sums(values, weights):
        sums = []
        for t in range(0, BLOCK, 2):
            both = jnp.concatenate(
                [
                    jnp.concatenate([weights[t], none], axis=1),
                    jnp.concatenate([none, weights[t + 1]], axis=1),
                ],
                axis=0,
            )
            result = matmul(values[:, t * agents : (t + 2) * agents], both)
            sums += [result[:, :width], result[:, width:]]
        return sums

    def gather_heads(sums):
        heads = []
        for h in range(HEADS):
            band = [value[h * head_size : (h + 1) * head_size] for value in sums]
            result = band[(HEADS - 1 - h) % HEADS]
            for place in range(HEADS - 1):
                result = jnp.where(blocks == place, band[(place - h) % HEADS], result)
            heads.append(pltpu.roll(result, width - h * pair, 1) if h else result)
        return jnp.concatenate(heads, axis=0).T.astype(jnp.bfloat16)

    def rotated_heads(query, t):
        return jnp.concatenate([query * masks[(place - t) % HEADS] for place in range(HEADS)], axis=0)

    def cross_group(firsts, target):
        rows = [slab[pl.ds(first, BLOCK)] for first in firsts]
        normed = [normalized(block.reshape(BLOCK * agents, width)) for block in rows]
        keys = [matmul(block, wc[:, width : 2 * width]).astype(jnp.bfloat16) for block in normed]
        own = [block.reshape(BLOCK, agents, width)[:, :pair].reshape(BLOCK * pair, width) for block in normed]
        queries = [matmul(block, wc[:, :width]).astype(jnp.bfloat16) for block in own]
        values = [matmul(wvt[...], block, NT).astype(jnp.bfloat16) for block in normed]
        scores = [
            [
                matmul(
                    key[t * agents : (t + 1) * agents],
                    rotated_heads(query[t * pair : (t + 1) * pair], t),
                    NT,
                )
                for t in range(BLOCK)
            ]
            for key, query in zip(keys, queries)
        ]
        weights = [[softmax_columns(score) for score in block] for block in scores]
        sums = [pair_sums(value, weight) for value, weight in zip(values, weights)]
        attended = [gather_heads(block) for block in sums]
        update = matmul(jnp.concatenate(attended, axis=0), wco[...])
        for j, first in enumerate(firsts):
            added = update[j * BLOCK * pair : (j + 1) * BLOCK * pair].reshape(BLOCK, pair, width)
            final = (rows[j][:, :pair].astype(jnp.float32) + added).astype(jnp.bfloat16)
            out[pl.ds(target + j * BLOCK, BLOCK)] = final[:, :ag_dev]
            sib_out[pl.ds(first, BLOCK)] = final[:, ag_dev:]

    def cross_piece(piece, carry):
        for copy in mix_arrivals(piece):
            copy.wait_recv()

        start = (chunks - 1 - piece // PARTS) * chunk + core * half + piece % PARTS * part

        def cross_blocks(i, inner):
            cross_group([piece * part + (i * BLOCKS + j) * BLOCK for j in range(BLOCKS)], start + i * BLOCKS * BLOCK)
            return inner

        lax.fori_loop(0, part // (BLOCK * BLOCKS), cross_blocks, 0)
        result_copy(piece, core).start()
        return carry

    wvt[...] = wc[:, 2 * width :].astype(jnp.float32).T.astype(jnp.bfloat16)
    lax.fori_loop(0, pieces, cross_piece, 0)

    def drain(k, carry):
        halo_copy(k).wait_send()
        for p in range(PARTS):
            for copy in mix_copies(k, p):
                copy.wait_send()
            piece = k * PARTS + p
            result_copy(piece, core).wait_send()
            result_copy(piece, 1 - core).wait_recv()
        return carry

    lax.fori_loop(0, chunks, drain, 0)


def local(panel, w_tqkv, w_tout, w_cqkv, w_cout):
    tm_dev, ag_dev, width = panel.shape
    chunk = 64
    chunks = tm_dev // chunk
    half = chunk // 2
    pieces = chunks * PARTS
    agents = ag_dev * lax.axis_size("agent")
    rows = WINDOW + tm_dev + (128 - chunk)
    bf16, f32 = jnp.bfloat16, jnp.float32
    any_spec = pl.BlockSpec(memory_space=pl.ANY)
    return pl.pallas_call(
        functools.partial(kernel, tm_axis="tm", agent_axis="agent", chunk=chunk),
        out_shape=pltpu.VMEM(panel.shape, bf16),
        in_specs=[any_spec] * 5,
        out_specs=pl.BlockSpec(memory_space=pltpu.VMEM),
        scratch_shapes=[
            pltpu.VMEM(panel.shape, bf16),
            pltpu.VMEM(panel.shape, bf16),
            pltpu.VMEM(w_tqkv.shape, bf16),
            pltpu.VMEM(w_tout.shape, bf16),
            pltpu.VMEM(w_cqkv.shape, bf16),
            pltpu.VMEM(w_cout.shape, bf16),
            pltpu.VMEM((chunk * ag_dev, width), f32),
            pltpu.VMEM((ag_dev, tm_dev, width), bf16),
            pltpu.VMEM((ag_dev, rows, width), bf16),
            pltpu.VMEM((ag_dev, rows, width), bf16),
            pltpu.VMEM((chunk * ag_dev, width), f32),
            pltpu.VMEM(panel.shape, bf16),
            pltpu.VMEM((chunks * half, agents, width), bf16),
            pltpu.VMEM((width, width), bf16),
            pltpu.VMEM((chunks * half, ag_dev, width), bf16),
            pltpu.SemaphoreType.DMA((5,)),
            pltpu.SemaphoreType.DMA((chunks,)),
            pltpu.SemaphoreType.DMA((chunks,)),
            pltpu.SemaphoreType.DMA((pieces, 3)),
            pltpu.SemaphoreType.DMA((pieces, 3)),
            pltpu.SemaphoreType.DMA((pieces,)),
            pltpu.SemaphoreType.DMA((pieces,)),
        ],
        compiler_params=pltpu.CompilerParams(
            collective_id=0, has_side_effects=True, vmem_limit_bytes=56 * 2**20
        ),
        name="axial_block",
    )(panel, w_tqkv, w_tout, w_cqkv, w_cout)


def solution(mesh):
    in_specs = (P("tm", "agent", None), P(), P(), P(), P())
    out_specs = P("tm", "agent", None)
    return jax.shard_map(local, mesh=mesh, in_specs=in_specs, out_specs=out_specs, check_vma=False)
```

```python
import functools
import math

import jax
import jax.numpy as jnp
from jax import lax
from jax.experimental import pallas as pl
from jax.experimental.pallas import tpu as pltpu
from jax.sharding import PartitionSpec as P

HEADS = 4
WINDOW = 256
EPSILON = 1e-06
UNROLL = 4
PARTS = 2
BLOCK = 4
BLOCKS = 4
MESH = pl.DeviceIdType.MESH
NT = (((1,), (1,)), ((), ()))
NN = (((1,), (0,)), ((), ()))


def matmul(left, right, dims=NN):
    return lax.dot_general(left, right, dims, preferred_element_type=jnp.float32)


def normalized(values):
    widened = values.astype(jnp.float32)
    scale = lax.rsqrt(jnp.mean(widened * widened, axis=-1, keepdims=True) + EPSILON)
    return (widened * scale).astype(jnp.bfloat16)


def by_head(values, masks):
    return jnp.concatenate([values * mask for mask in masks], axis=0)


def pick_heads(stacked, rows, picks):
    blocks = [stacked[h * rows : (h + 1) * rows] for h in range(HEADS)]
    result = blocks[-1]
    for pick, block in zip(picks, blocks):
        result = jnp.where(pick, block, result)
    return result


def kernel(
    x_hbm, wt_hbm, wto_hbm, wc_hbm, wco_hbm, out,
    xv, halo, wt, wto, wc, wco, wide, q1, k1, v1, upd, mixed, slab, wvt, sib_out,
    load_sem, halo_send, halo_recv, mix_send, mix_recv, res_send, res_recv,
    *, tm_axis, agent_axis, chunk,
):
    tm_dev, ag_dev, width = xv.shape
    chunks = tm_dev // chunk
    half = chunk // 2
    part = half // PARTS
    pieces = chunks * PARTS
    agents = slab.shape[1]
    pair = 2 * ag_dev
    head_size = width // HEADS
    factor = math.log2(math.e) * head_size ** (-0.5)
    tm = lax.axis_index(tm_axis)
    ag = lax.axis_index(agent_axis)
    tm_count = lax.axis_size(tm_axis)
    side = ag // 2
    core = ag % 2
    ahead = (lax.rem(tm + 1, tm_count), ag)
    behind = (lax.rem(tm + tm_count - 1, tm_count), ag)
    sibling = (tm, side * 2 + 1 - core)
    far = [(tm, (1 - side) * 2 + j) for j in range(2)]

    loads = [
        pltpu.make_async_copy(src, dst, load_sem.at[i])
        for i, (src, dst) in enumerate(
            [(x_hbm, xv), (wt_hbm, wt), (wto_hbm, wto), (wc_hbm, wc), (wco_hbm, wco)]
        )
    ]
    for load in loads:
        load.start()

    barrier = pltpu.get_barrier_semaphore()
    for peer in (behind, sibling, far[0], far[1]):
        pl.semaphore_signal(barrier, inc=1, device_id=peer, device_id_type=MESH)
    pl.semaphore_wait(barrier, 4)

    def halo_copy(c):
        rows = pl.ds(c * chunk, chunk)
        return pltpu.make_async_remote_copy(
            src_ref=x_hbm.at[rows], dst_ref=halo.at[rows],
            send_sem=halo_send.at[c], recv_sem=halo_recv.at[c],
            device_id=ahead, device_id_type=MESH,
        )

    has_ahead = tm < tm_count - 1
    has_behind = tm > 0

    @pl.when(has_ahead)
    def _():
        for c in reversed(range(chunks)):
            halo_copy(c).start()

    @pl.when(jnp.logical_not(has_behind))
    def _():
        halo[...] = jnp.zeros(halo.shape, halo.dtype)

    lanes = lax.broadcasted_iota(jnp.int32, (1, width), 1) // head_size
    masks = [(lanes == h).astype(jnp.bfloat16) for h in range(HEADS)]
    picks = [lanes == h for h in range(HEADS - 1)]
    later = (
        lax.broadcasted_iota(jnp.int32, (HEADS * chunk, 128), 1)
        <= lax.broadcasted_iota(jnp.int32, (HEADS * chunk, 128), 0) % chunk
    )

    for load in loads[:2]:
        load.wait()

    group = 4

    def spread(src, start):
        def piece(i, carry):
            rows = normalized(src[pl.ds(start + i * 8, 8)].reshape(8 * ag_dev, width))
            wide[pl.ds(pl.multiple_of(i * 8 * ag_dev, 8 * ag_dev), 8 * ag_dev), :] = rows.astype(jnp.float32)
            return carry

        lax.fori_loop(0, chunk // 8, piece, 0)

    def project(row0, is_halo, start):
        def agents4(g, carry):
            parts = []
            for i in range(group):
                rows = wide[pl.ds(g * group + i, chunk, stride=ag_dev), :]
                parts.append(rows.astype(jnp.bfloat16))
            result = matmul(jnp.concatenate(parts, 0), wt[...])
            keys = result[:, width : 2 * width].astype(jnp.bfloat16)
            vals = result[:, 2 * width :].astype(jnp.bfloat16)
            at = pl.ds(g * group, group)
            k1[at, pl.ds(row0, chunk), :] = keys.reshape(group, chunk, width)
            v1[at, pl.ds(row0, chunk), :] = vals.reshape(group, chunk, width)
            if not is_halo:
                q1[at, pl.ds(start, chunk), :] = result[:, :width].astype(jnp.bfloat16).reshape(group, chunk, width)
            return carry

        lax.fori_loop(0, ag_dev // group, agents4, 0)

    extra = k1.shape[1] - 2 * tm_dev
    if extra:
        k1[:, pl.ds(2 * tm_dev, extra), :] = jnp.zeros((ag_dev, extra, width), jnp.bfloat16)
        v1[:, pl.ds(2 * tm_dev, extra), :] = jnp.zeros((ag_dev, extra, width), jnp.bfloat16)

    def own_chunk(c, carry):
        start = pl.multiple_of(c * chunk, chunk)
        spread(xv, start)
        project(pl.multiple_of(tm_dev + start, chunk), False, start)
        return carry

    lax.fori_loop(0, chunks, own_chunk, 0)
    for load in loads[2:]:
        load.wait()

    def mix_copies(k, p):
        start = (chunks - 1 - k) * chunk + p * part
        piece = k * PARTS + p
        away = pl.multiple_of(pair + core * ag_dev, ag_dev)
        result = []
        for i, (peer, target, slot) in enumerate(
            [(sibling, 1 - core, ag_dev), (far[0], 0, away), (far[1], 1, away)]
        ):
            result.append(
                pltpu.make_async_remote_copy(
                    src_ref=mixed.at[pl.ds(start + target * half, part)],
                    dst_ref=slab.at[pl.ds(piece * part, part), pl.ds(slot, ag_dev)],
                    send_sem=mix_send.at[piece, i],
                    recv_sem=mix_recv.at[piece, 0 if i == 0 else 1 + core],
                    device_id=peer, device_id_type=MESH,
                )
            )
        return result

    def mix_arrivals(piece):
        return [
            pltpu.make_async_remote_copy(
                src_ref=mixed.at[pl.ds(0, part)],
                dst_ref=slab.at[pl.ds(piece * part, part), pl.ds((i + 1) * ag_dev, ag_dev)],
                send_sem=mix_send.at[piece, i], recv_sem=mix_recv.at[piece, i],
                device_id=peer, device_id_type=MESH,
            )
            for i, peer in enumerate([sibling, far[0], far[1]])
        ]

    def temporal_chunk(k, carry):
        c = chunks - 1 - k
        start = pl.multiple_of(c * chunk, chunk)

        @pl.when(has_behind)
        def _():
            halo_copy(c).wait_recv()

        spread(halo, start)
        project(start, True, start)

        columns = lax.broadcasted_iota(jnp.int32, (1, WINDOW), 1) + start
        absent = jnp.where((tm == 0) & (columns < WINDOW), -1e30, 0.0)

        def temporal_agents(i, inner):
            ids = [i * UNROLL + j for j in range(UNROLL)]
            scores = [
                matmul(by_head(q1[a, pl.ds(start, chunk), :], masks), k1[a, pl.ds(start, WINDOW + 128), :], NT)
                for a in ids
            ]
            weights = []
            for score in scores:
                edge = jnp.where(later, score[:, WINDOW:], score[:, :128] + absent[:, :128])
                middle = score[:, 128:WINDOW] + absent[:, 128:]
                top = jnp.max(jnp.maximum(edge, middle), axis=1, keepdims=True)
                edge = jnp.exp2((edge - top) * factor)
                middle = jnp.exp2((middle - top) * factor)
                share = 1.0 / jnp.sum(edge + middle, axis=1, keepdims=True)
                edge = edge * share
                middle = middle * share
                weights.append(
                    jnp.concatenate(
                        [jnp.where(later, 0.0, edge), middle, jnp.where(later, edge, 0.0)], axis=1
                    ).astype(jnp.bfloat16)
                )
            sums = [matmul(weight, v1[a, pl.ds(start, WINDOW + 128), :]) for a, weight in zip(ids, weights)]
            attended = [pick_heads(value, chunk, picks).astype(jnp.bfloat16) for value in sums]
            update = matmul(jnp.concatenate(attended, 0), wto[...])
            for j, a in enumerate(ids):
                upd[pl.ds(a, chunk, stride=ag_dev), :] = update[j * chunk : (j + 1) * chunk]
            return inner

        lax.fori_loop(0, ag_dev // UNROLL, temporal_agents, 0)

        def add_piece(i, inner):
            rows = pl.ds(start + i * 8, 8)
            update = upd[pl.ds(pl.multiple_of(i * 8 * ag_dev, 8 * ag_dev), 8 * ag_dev), :]
            mixed[rows] = (xv[rows].astype(jnp.float32) + update.reshape(8, ag_dev, width)).astype(jnp.bfloat16)
            return inner

        lax.fori_loop(0, chunk // 8, add_piece, 0)
        slab[pl.ds(k * half, half), pl.ds(0, ag_dev), :] = mixed[pl.ds(start + core * half, half)]
        for p in range(PARTS):
            for copy in mix_copies(k, p):
                copy.start()
        return carry

    lax.fori_loop(0, chunks, temporal_chunk, 0)

    def result_copy(piece, owner):
        start = (chunks - 1 - piece // PARTS) * chunk + owner * half + piece % PARTS * part
        return pltpu.make_async_remote_copy(
            src_ref=sib_out.at[pl.ds(piece * part, part)], dst_ref=out.at[pl.ds(start, part)],
            send_sem=res_send.at[piece], recv_sem=res_recv.at[piece],
            device_id=sibling, device_id_type=MESH,
        )

    blocks = lax.broadcasted_iota(jnp.int32, (1, width), 1) // pair
    none = jnp.zeros((agents, width), jnp.bfloat16)

    def softmax_columns(scores):
        powers = jnp.exp2((scores - jnp.max(scores, axis=0, keepdims=True)) * factor)
        share = 1.0 / jnp.sum(powers, axis=0, keepdims=True)
        return (powers * share).astype(jnp.bfloat16)

    def pair_sums(values, weights):
        sums = []
        for t in range(0, BLOCK, 2):
            both = jnp.concatenate(
                [
                    jnp.concatenate([weights[t], none], axis=1),
                    jnp.concatenate([none, weights[t + 1]], axis=1),
                ],
                axis=0,
            )
            result = matmul(values[:, t * agents : (t + 2) * agents], both)
            sums += [result[:, :width], result[:, width:]]
        return sums

    def gather_heads(sums):
        heads = []
        for h in range(HEADS):
            band = [value[h * head_size : (h + 1) * head_size] for value in sums]
            result = band[(HEADS - 1 - h) % HEADS]
            for place in range(HEADS - 1):
                result = jnp.where(blocks == place, band[(place - h) % HEADS], result)
            heads.append(pltpu.roll(result, width - h * pair, 1) if h else result)
        return jnp.concatenate(heads, axis=0).T.astype(jnp.bfloat16)

    def rotated_heads(query, t):
        return jnp.concatenate([query * masks[(place - t) % HEADS] for place in range(HEADS)], axis=0)

    def cross_group(firsts, target):
        rows = [slab[pl.ds(first, BLOCK)] for first in firsts]
        normed = [normalized(block.reshape(BLOCK * agents, width)) for block in rows]
        keys = [matmul(block, wc[:, width : 2 * width]).astype(jnp.bfloat16) for block in normed]
        own = [block.reshape(BLOCK, agents, width)[:, :pair].reshape(BLOCK * pair, width) for block in normed]
        queries = [matmul(block, wc[:, :width]).astype(jnp.bfloat16) for block in own]
        values = [matmul(wvt[...], block, NT).astype(jnp.bfloat16) for block in normed]
        scores = [
            [
                matmul(
                    key[t * agents : (t + 1) * agents],
                    rotated_heads(query[t * pair : (t + 1) * pair], t),
                    NT,
                )
                for t in range(BLOCK)
            ]
            for key, query in zip(keys, queries)
        ]
        weights = [[softmax_columns(score) for score in block] for block in scores]
        sums = [pair_sums(value, weight) for value, weight in zip(values, weights)]
        attended = [gather_heads(block) for block in sums]
        update = matmul(jnp.concatenate(attended, axis=0), wco[...])
        for j, first in enumerate(firsts):
            added = update[j * BLOCK * pair : (j + 1) * BLOCK * pair].reshape(BLOCK, pair, width)
            final = (rows[j][:, :pair].astype(jnp.float32) + added).astype(jnp.bfloat16)
            out[pl.ds(target + j * BLOCK, BLOCK)] = final[:, :ag_dev]
            sib_out[pl.ds(first, BLOCK)] = final[:, ag_dev:]

    def cross_piece(piece, carry):
        for copy in mix_arrivals(piece):
            copy.wait_recv()

        start = (chunks - 1 - piece // PARTS) * chunk + core * half + piece % PARTS * part

        def cross_blocks(i, inner):
            cross_group([piece * part + (i * BLOCKS + j) * BLOCK for j in range(BLOCKS)], start + i * BLOCKS * BLOCK)
            return inner

        lax.fori_loop(0, part // (BLOCK * BLOCKS), cross_blocks, 0)
        result_copy(piece, core).start()
        return carry

    wvt[...] = wc[:, 2 * width :].astype(jnp.float32).T.astype(jnp.bfloat16)
    lax.fori_loop(0, pieces, cross_piece, 0)

    def drain(k, carry):
        @pl.when(has_ahead)
        def _():
            halo_copy(k).wait_send()

        for p in range(PARTS):
            for copy in mix_copies(k, p):
                copy.wait_send()
            piece = k * PARTS + p
            result_copy(piece, core).wait_send()
            result_copy(piece, 1 - core).wait_recv()
        return carry

    lax.fori_loop(0, chunks, drain, 0)


def local(panel, w_tqkv, w_tout, w_cqkv, w_cout):
    tm_dev, ag_dev, width = panel.shape
    chunk = 64
    chunks = tm_dev // chunk
    half = chunk // 2
    pieces = chunks * PARTS
    agents = ag_dev * lax.axis_size("agent")
    rows = WINDOW + tm_dev + (128 - chunk)
    bf16, f32 = jnp.bfloat16, jnp.float32
    any_spec = pl.BlockSpec(memory_space=pl.ANY)
    return pl.pallas_call(
        functools.partial(kernel, tm_axis="tm", agent_axis="agent", chunk=chunk),
        out_shape=pltpu.VMEM(panel.shape, bf16),
        in_specs=[any_spec] * 5,
        out_specs=pl.BlockSpec(memory_space=pltpu.VMEM),
        scratch_shapes=[
            pltpu.VMEM(panel.shape, bf16),
            pltpu.VMEM(panel.shape, bf16),
            pltpu.VMEM(w_tqkv.shape, bf16),
            pltpu.VMEM(w_tout.shape, bf16),
            pltpu.VMEM(w_cqkv.shape, bf16),
            pltpu.VMEM(w_cout.shape, bf16),
            pltpu.VMEM((chunk * ag_dev, width), f32),
            pltpu.VMEM((ag_dev, tm_dev, width), bf16),
            pltpu.VMEM((ag_dev, rows, width), bf16),
            pltpu.VMEM((ag_dev, rows, width), bf16),
            pltpu.VMEM((chunk * ag_dev, width), f32),
            pltpu.VMEM(panel.shape, bf16),
            pltpu.VMEM((chunks * half, agents, width), bf16),
            pltpu.VMEM((width, width), bf16),
            pltpu.VMEM((chunks * half, ag_dev, width), bf16),
            pltpu.SemaphoreType.DMA((5,)),
            pltpu.SemaphoreType.DMA((chunks,)),
            pltpu.SemaphoreType.DMA((chunks,)),
            pltpu.SemaphoreType.DMA((pieces, 3)),
            pltpu.SemaphoreType.DMA((pieces, 3)),
            pltpu.SemaphoreType.DMA((pieces,)),
            pltpu.SemaphoreType.DMA((pieces,)),
        ],
        compiler_params=pltpu.CompilerParams(
            collective_id=0, has_side_effects=True, vmem_limit_bytes=56 * 2**20
        ),
        name="axial_block",
    )(panel, w_tqkv, w_tout, w_cqkv, w_cout)


def solution(mesh):
    in_specs = (P("tm", "agent", None), P(), P(), P(), P())
    out_specs = P("tm", "agent", None)
    return jax.shard_map(local, mesh=mesh, in_specs=in_specs, out_specs=out_specs, check_vma=False)
```
